32 devices in a mesh: lat: 8 (over y, x, core), lon: 4 (over z).
Axes of the slice: x: 2, y: 2, z: 4, core: 2. Of those that a mesh axis runs over, the one named last changes fastest.
Arguments:
- snapshots: float32 [1024, 128, 512], P(None, 'lat', 'lon'), may hold values from -60 to 60
- land_sea: int32 [128, 512], P('lat', 'lon'), may hold values 0 or 1
- penalty: float32 [128, 512], P('lat', 'lon'), may hold values from 0.003 to 0.03
- initial_basis: float32 [64, 128, 512], P(None, 'lat', 'lon'), may hold values from -6 to 6
Outputs:
- leading_basis: float32 [64, 128, 512], P(None, 'lat', 'lon')
- rayleigh_matrix: float32 [64, 64], replicated
The draws below stay inside these ranges and needn't reach their ends.
All inputs are finite; a program needn't handle non-finite values. No bound on the sum of `land_sea` on one device may be relied on, other than what follows from the above.
Results may differ from the reference program's by a relative error of at most 0.0003.
Values sent between devices are 32-bit elements; how exact they have to be, the bound alone decides.
A program may use at most 64 MiB of HBM per device.

```python
import math
import jax
import jax.numpy as jnp
from jax import lax

K = 64
NSNAP = 1024
STEPS = 2
NLAT = 128
NLON = 512
NPTS = 65536


def draw_snapshots(key, part):
    streams = jax.random.split(jax.random.fold_in(key, 7), 9)
    snapshot_scale = 10.0 ** jax.random.uniform(streams[0], (NSNAP, 1, 1), dtype=jnp.float32) / 4.637
    point_scale = 10.0 ** jax.random.uniform(streams[1], (1, NLAT, NLON), dtype=jnp.float32) / 4.637
    latitude_ramp = (1.0 + 2.0 * jnp.arange(NLAT, dtype=jnp.float32) / max(NLAT - 1, 1)).reshape(1, NLAT, 1) / 2.082
    lat_frac = (jnp.arange(NLAT, dtype=jnp.float32) / NLAT).reshape(1, NLAT, 1)
    lon_frac = (jnp.arange(NLON, dtype=jnp.float32) / NLON).reshape(1, 1, NLON)
    wave_lat = jax.random.randint(streams[4], (4,), 1, 5).astype(jnp.float32)
    wave_lon = jax.random.randint(streams[5], (4,), 1, 5).astype(jnp.float32)
    phases = jax.random.uniform(streams[6], (4,), dtype=jnp.float32, minval=0.0, maxval=2.0 * math.pi)
    strength = 6.0 * 5.0 ** jax.random.uniform(streams[7], (4,), dtype=jnp.float32)
    amplitude = jnp.sqrt(2.0 * strength / NSNAP)
    series = jnp.clip(jax.random.normal(streams[8], (4, NSNAP), dtype=jnp.float32), -3.0, 3.0)
    modes_sum = jnp.zeros((NSNAP, NLAT, NLON), jnp.float32)
    for mode in range(4):
        pattern = jnp.cos(2.0 * math.pi * (wave_lat[mode] * lat_frac + wave_lon[mode] * lon_frac) + phases[mode])
        modes_sum = modes_sum + (amplitude[mode] * series[mode]).reshape(NSNAP, 1, 1) * pattern
    values = jnp.clip(jax.random.normal(streams[2], (NSNAP, NLAT, NLON), dtype=jnp.float32), -6.0, 6.0)
    return ((values * snapshot_scale * point_scale + modes_sum) * latitude_ramp).astype(jnp.float32)


def place_ends(entries, own_key, low, high):
    spot = [jax.random.randint(jax.random.fold_in(own_key, axis), (), 0, length) for axis, length in enumerate(entries.shape)]
    longest = entries.shape.index(max(entries.shape))
    next_to = spot[:longest] + [(spot[longest] + 1) % entries.shape[longest]] + spot[longest + 1:]
    return entries.at[tuple(spot)].set(low).at[tuple(next_to)].set(high)


def shard_levels(key, extent, cuts, least, largest):
    level, own = 1.0, jax.random.fold_in(key, 6)
    for position, blocks in cuts:
        steps = jnp.exp(jax.random.uniform(jax.random.fold_in(own, position), (blocks,), jnp.float32, least / len(cuts), largest / len(cuts)))
        level = level * jnp.repeat(steps, extent[position] // blocks).reshape([-1 if axis == position else 1 for axis in range(len(extent))])
    return level


def centred(stream_key, shape, spread, most, cuts=(), held_as=jnp.bfloat16):
    entries = spread * jax.random.normal(stream_key, shape, jnp.float32)
    if cuts:
        entries = entries * shard_levels(stream_key, shape, cuts, -0.22, 0.18)
    return jnp.clip(entries, -most, most).astype(held_as)


def setup_inputs(seed: int = 0) -> dict:
    arg_keys = jax.random.split(jax.random.key(seed), 5)
    return {
        "snapshots": draw_snapshots(jax.random.fold_in(arg_keys[4], 71), 0),
        "land_sea": place_ends((jax.random.randint(arg_keys[1], (NLAT, NLON), 0, 4) < 3).astype(jnp.int32), jax.random.fold_in(arg_keys[1], 1), 0, 1),
        "penalty": jnp.clip(jnp.exp(math.log(0.03) - 2.3025851 * jax.random.uniform(arg_keys[2], (NLAT, NLON), jnp.float32) ** shard_levels(arg_keys[2], (NLAT, NLON), ((0, 8), (1, 4)), -0.2, 0.2)), 0.003, 0.03),
        "initial_basis": centred(arg_keys[3], (K, NLAT, NLON), 1.0, 6.0, ((1, 8), (2, 4)), jnp.float32),
    }


def apply_operator(current_basis, snapshots, ocean_mask, penalty):
    masked_field = current_basis * ocean_mask
    coeffs = jnp.einsum('tab,kab->tk', snapshots, masked_field, precision=lax.Precision.HIGHEST)
    expanded = jnp.einsum('tab,tk->kab', snapshots, coeffs, precision=lax.Precision.HIGHEST)
    padded = jnp.pad(masked_field, ((0, 0), (1, 1), (1, 1)))
    neighbours = padded[:, 2:, 1:-1] + padded[:, :-2, 1:-1] + padded[:, 1:-1, 2:] + padded[:, 1:-1, :-2]
    return ocean_mask * (expanded / NPTS + penalty * (neighbours - 4.0 * masked_field))

def inner_products(left_field, right_field):
    return jnp.einsum('kab,jab->kj', left_field, right_field, precision=lax.Precision.HIGHEST)

def reference(snapshots, land_sea, penalty, initial_basis):
    ocean_mask = land_sea.astype(jnp.float32)
    current_basis = initial_basis * ocean_mask
    for iteration in range(STEPS):
        applied = apply_operator(current_basis, snapshots, ocean_mask, penalty)
        moments = inner_products(applied, applied) / NPTS
        factor = jnp.linalg.cholesky(moments)
        solved = jax.scipy.linalg.solve_triangular(factor, applied.reshape(K, -1), lower=True)
        current_basis = solved.reshape(applied.shape)
    final_image = apply_operator(current_basis, snapshots, ocean_mask, penalty)
    rayleigh_matrix = inner_products(current_basis, final_image) / NPTS
    return (current_basis, rayleigh_matrix)
```

```python
import functools

import jax
import jax.numpy as jnp
from jax import lax
from jax.experimental import pallas as pl
from jax.experimental.pallas import tpu as pltpu
from jax.sharding import PartitionSpec as P

STEPS = 2
MESH = pl.DeviceIdType.MESH
F32 = jnp.float32
BF16 = jnp.bfloat16
NT = (((1,), (1,)), ((), ()))
NN = (((1,), (0,)), ((), ()))


def dot_low(a, b, dims):
    return lax.dot_general(a, b, dims, preferred_element_type=F32)


def dot_full(a, b, dims):
    return lax.dot_general(
        a, b, dims, precision=lax.Precision.HIGHEST, preferred_element_type=F32
    )


def split(x):
    high = x.astype(BF16)
    return high, (x - high.astype(F32)).astype(BF16)


def inverse_factor(gram):
    k = gram.shape[0]
    rows = lax.broadcasted_iota(jnp.int32, (k, k), 0)
    cols = lax.broadcasted_iota(jnp.int32, (k, k), 1)
    eye = jnp.where(rows == cols, 1.0, 0.0).astype(F32)
    work = jnp.concatenate([gram, eye], axis=1)
    blocks = [work[8 * i:8 * i + 8] for i in range(k // 8)]
    sub = lax.broadcasted_iota(jnp.int32, (8, 2 * k), 0)
    pivots = [jnp.zeros((8, 2 * k), F32) for _ in range(k // 8)]
    for j in range(k):
        own, at = j // 8, j % 8
        row = jnp.broadcast_to(blocks[own][at:at + 1, :], (8, 2 * k))
        columns = [
            jnp.broadcast_to(blocks[i][:, j:j + 1], (8, 2 * k)) for i in range(own, k // 8)
        ]
        pivot = jnp.broadcast_to(columns[0][at:at + 1, :], (8, 2 * k))
        pivots[own] = jnp.where(sub == at, pivot, pivots[own])
        scaled = row * (1.0 / pivot)
        for i in range(own, k // 8):
            column = columns[i - own]
            if i == own:
                column = jnp.where(sub > at, column, 0.0)
            blocks[i] = blocks[i] - column * scaled
    done = [blocks[i] * (1.0 / jnp.sqrt(pivots[i])) for i in range(k // 8)]
    return jnp.concatenate(done, axis=0)[:, k:]


def kernel(
    n, m, points, s_hbm, land_ref, pen_ref, v_hbm, out_hbm, ray_ref,
    s_full, s_high, s_mid, field0, field1, field2, lap_ref, out_buf, v_split, acc,
    cbuf, rs, zr, fin, gl, gz, edge, halo,
    s_sem, v_sem, o_sem, rs_s, rs_r, z_s, z_r, ag_s, ag_r, gl_s, gl_r, gz_s, gz_r, h_s, h_r,
):
    lat = lax.axis_index("lat")
    lon = lax.axis_index("lon")
    t_count, a_count, b_count = s_hbm.shape
    k = v_hbm.shape[0]
    fields = (field0, field1, field2)
    shard = cbuf.shape[1] // n
    inverse_points = 1.0 / points
    pending = []

    def part(a):
        return pl.ds(a * b_count, b_count)

    loads = []
    for a in range(a_count):
        loads.append(pltpu.make_async_copy(v_hbm.at[:, a, :], out_buf.at[:, part(a)], v_sem.at[a]))
    for a in range(a_count):
        loads.append(pltpu.make_async_copy(s_hbm.at[:, a, :], s_full.at[:, part(a)], s_sem.at[a]))
    for copy in loads:
        copy.start()

    barrier = pltpu.get_barrier_semaphore()
    for d in range(1, n):
        pl.semaphore_signal(
            barrier, inc=1, device_id=(lax.rem(lat + d, n), lon), device_id_type=MESH
        )
    for e in range(1, m):
        pl.semaphore_signal(
            barrier, inc=1, device_id=(lat, lax.rem(lon + e, m)), device_id_type=MESH
        )
    pl.semaphore_wait(barrier, n + m - 2)

    def send(src, dst, s_s, s_r, where):
        copy = pltpu.make_async_remote_copy(
            src_ref=src, dst_ref=dst, send_sem=s_s, recv_sem=s_r,
            device_id=where, device_id_type=MESH,
        )
        copy.start()
        pending.append(copy)
        return copy

    def to_lat(d):
        return (lax.rem(lat + d, n), lon)

    def to_lon(e):
        return (lat, lax.rem(lon + e, m))

    lane = lax.broadcasted_iota(jnp.int32, (k, b_count), 1)

    def mask_row(a):
        return land_ref[a:a + 1, :].astype(F32)

    def start_halo(r):
        x = fields[r]
        packed = jnp.zeros((k, b_count), F32)
        for a in range(a_count):
            block = x[:, a * b_count:(a + 1) * b_count]
            low = block if a == 0 else pltpu.roll(block, a, axis=1)
            high = pltpu.roll(block, a_count + a + 1, axis=1)
            packed = jnp.where(lane == a, low, packed)
            packed = jnp.where(lane == a_count + a, high, packed)
        edge[r] = packed
        return [
            send(x.at[:, part(a_count - 1)], halo.at[r, 0], h_s.at[r, 0], h_r.at[r, 0], to_lat(1)),
            send(x.at[:, part(0)], halo.at[r, 1], h_s.at[r, 1], h_r.at[r, 1], to_lat(n - 1)),
            send(edge.at[r], halo.at[r, 2], h_s.at[r, 2], h_r.at[r, 2], to_lon(1)),
            send(edge.at[r], halo.at[r, 3], h_s.at[r, 3], h_r.at[r, 3], to_lon(m - 1)),
        ]

    def laplacian(r, copies):
        for copy in copies:
            copy.wait_recv()
        x = fields[r]
        above = jnp.where(lat > 0, halo[r, 0], 0.0)
        below = jnp.where(lat < n - 1, halo[r, 1], 0.0)
        west = jnp.where(lon > 0, halo[r, 2], 0.0)
        east = jnp.where(lon < m - 1, halo[r, 3], 0.0)
        for a in range(a_count):
            block = x[:, a * b_count:(a + 1) * b_count]
            up = above if a == 0 else x[:, (a - 1) * b_count:a * b_count]
            down = below if a == a_count - 1 else x[:, (a + 1) * b_count:(a + 2) * b_count]
            left = jnp.where(
                lane == 0, pltpu.roll(west, b_count - a_count - a, axis=1),
                pltpu.roll(block, 1, axis=1),
            )
            right = jnp.where(
                lane == b_count - 1, pltpu.roll(east, b_count - 1 - a, axis=1),
                pltpu.roll(block, b_count - 1, axis=1),
            )
            total = (down + up + right + left) - 4.0 * block
            lap_ref[:, a * b_count:(a + 1) * b_count] = total * pen_ref[a:a + 1, :]

    def store_field(r, a, value):
        x = value * mask_row(a)
        high, mid = split(x)
        at = slice(a * b_count, (a + 1) * b_count)
        fields[r][:, at] = x
        v_split[:k, at] = high
        v_split[k:, at] = mid

    def store_coeffs(r, block, value):
        for w in range(value.shape[1] // b_count):
            row = (block * (value.shape[1] // b_count) + w) * k
            cbuf[r, row:row + k, :] = value[:, w * b_count:(w + 1) * b_count]

    def start_scatter(r):
        copies = []
        for d in range(1, n):
            there = lax.rem(lat + d, n)
            rows = pl.ds(pl.multiple_of(there * shard, shard), shard)
            copies.append(
                send(cbuf.at[r, rows], rs.at[r, d], rs_s.at[r, d], rs_r.at[r, d], to_lat(d))
            )
        return copies

    def own_rows():
        return pl.ds(pl.multiple_of(lat * shard, shard), shard)

    def finish_scatter(r, copies):
        total = cbuf[r, own_rows(), :]
        for d, copy in enumerate(copies):
            copy.wait_recv()
            total = total + rs[r, d + 1]
        zr[r, lon] = total
        return [
            send(zr.at[r, lon], zr.at[r, lon], z_s.at[r, e], z_r.at[r, e], to_lon(e))
            for e in range(1, m)
        ]

    def start_gather(r, copies):
        for copy in copies:
            copy.wait_recv()
        total = zr[r, 0]
        for e in range(1, m):
            total = total + zr[r, e]
        fin[r, own_rows(), :] = total
        return [
            send(fin.at[r, own_rows()], fin.at[r, own_rows()], ag_s.at[r, d], ag_r.at[r, d], to_lat(d))
            for d in range(1, n)
        ]

    def finish_gather(r, copies):
        for copy in copies:
            copy.wait_recv()
        return jnp.concatenate(
            [fin[r, i * k:(i + 1) * k, :] for i in range(t_count // b_count)], axis=1
        )

    def start_gram(r, value):
        gl[r, lat] = value
        return [
            send(gl.at[r, lat], gl.at[r, lat], gl_s.at[r, d], gl_r.at[r, d], to_lat(d))
            for d in range(1, n)
        ]

    def middle_gram(r, copies):
        for copy in copies:
            copy.wait_recv()
        total = gl[r, 0]
        for d in range(1, n):
            total = total + gl[r, d]
        gz[r, lon] = total
        return [
            send(gz.at[r, lon], gz.at[r, lon], gz_s.at[r, e], gz_r.at[r, e], to_lon(e))
            for e in range(1, m)
        ]

    def finish_gram(r, copies):
        for copy in copies:
            copy.wait_recv()
        total = gz[r, 0]
        for e in range(1, m):
            total = total + gz[r, e]
        return total

    def project(r):
        width = 2 * b_count
        for block in range(t_count // width):
            rows = slice(block * width, (block + 1) * width)
            both = dot_low(v_split[...], s_high[rows, :], NT)
            rest = dot_low(v_split[:k, :], s_mid[rows, :], NT)
            store_coeffs(r, block, both[:k] + (both[k:] + rest))

    def expand(r, coeffs):
        high, mid = split(coeffs)
        stacked = jnp.concatenate([high, mid], axis=0)
        width = 2 * b_count
        for block in range(a_count // 2):
            at = slice(block * width, (block + 1) * width)
            both = dot_low(stacked, s_high[:, at], NN)
            rest = dot_low(high, s_mid[:, at], NN)
            value = (both[:k] + (both[k:] + rest)) * inverse_points + lap_ref[:, at]
            store_field(r, 2 * block, value[:, :b_count])
            store_field(r, 2 * block + 1, value[:, b_count:])

    for a in range(a_count):
        loads[a].wait()
        store_field(0, a, out_buf[:, a * b_count:(a + 1) * b_count])
    halo_copies = start_halo(0)
    width = 2 * b_count
    for block in range(a_count // 2):
        at = slice(block * width, (block + 1) * width)
        loads[a_count + 2 * block].wait()
        loads[a_count + 2 * block + 1].wait()
        high, mid = split(s_full[:, at])
        s_high[:, at] = high
        s_mid[:, at] = mid
        both = dot_low(v_split[:, at], high, NT)
        rest = dot_low(v_split[:k, at], mid, NT)
        value = both[:k] + (both[k:] + rest)
        if block == 0:
            acc[...] = value
        else:
            acc[...] += value
    store_coeffs(0, 0, acc[...])
    copies = start_scatter(0)
    laplacian(0, halo_copies)
    copies = finish_scatter(0, copies)
    copies = start_gather(0, copies)
    expand(1, finish_gather(0, copies))

    halo_copies = start_halo(1)
    x = field1[...]
    gram = dot_full(x, x, NT) * inverse_points
    gram_copies = start_gram(0, jnp.concatenate([gram, gram], axis=1))
    project(1)
    copies = start_scatter(1)
    gram_copies = middle_gram(0, gram_copies)
    laplacian(1, halo_copies)
    copies = finish_scatter(1, copies)
    inverse = inverse_factor(finish_gram(0, gram_copies)[:, :k])
    copies = start_gather(1, copies)
    lap_ref[...] = dot_full(inverse, lap_ref[...], NN)
    expand(2, dot_full(inverse, finish_gather(1, copies), NN))

    halo_copies = start_halo(2)
    project(2)
    copies = start_scatter(2)
    laplacian(2, halo_copies)
    x = field2[...]
    gram = dot_full(x, x, NT) * inverse_points
    rough = dot_full(x, lap_ref[...], NT)
    gram_copies = start_gram(1, jnp.concatenate([gram, rough], axis=1))
    copies = finish_scatter(2, copies)
    gram_copies = middle_gram(1, gram_copies)
    copies = start_gather(2, copies)
    both = finish_gram(1, gram_copies)
    inverse = inverse_factor(both[:, :k])
    stores = []
    for a in range(a_count):
        at = slice(a * b_count, (a + 1) * b_count)
        out_buf[:, at] = dot_full(inverse, field2[:, at], NN)
        copy = pltpu.make_async_copy(out_buf.at[:, part(a)], out_hbm.at[:, a, :], o_sem.at[a])
        copy.start()
        stores.append(copy)
    coeffs = finish_gather(2, copies)
    middle = dot_full(coeffs, coeffs, NT) * inverse_points + both[:, k:]
    ray_ref[...] = dot_full(dot_full(inverse, middle, NN), inverse, NT) * inverse_points
    for copy in stores:
        copy.wait()
    for copy in pending:
        copy.wait_send()


def local(snapshots, land_sea, penalty, initial_basis):
    n, m = lax.axis_size("lat"), lax.axis_size("lon")
    t, a, b = snapshots.shape
    k = initial_basis.shape[0]
    points = float(a * b * n * m)
    p = a * b
    rows = t * k // b
    shard = rows // n
    sem = pltpu.SemaphoreType.DMA
    vmem = pltpu.VMEM
    any_spec = pl.BlockSpec(memory_space=pl.ANY)
    vmem_spec = pl.BlockSpec(memory_space=pltpu.VMEM)
    return pl.pallas_call(
        functools.partial(kernel, n, m, points),
        out_shape=(
            jax.ShapeDtypeStruct((k, a, b), F32),
            jax.ShapeDtypeStruct((k, k), F32),
        ),
        in_specs=[any_spec, vmem_spec, vmem_spec, any_spec],
        out_specs=(any_spec, vmem_spec),
        scratch_shapes=[
            vmem((t, p), F32), vmem((t, p), BF16), vmem((t, p), BF16),
            vmem((k, p), F32), vmem((k, p), F32), vmem((k, p), F32),
            vmem((k, p), F32), vmem((k, p), F32), vmem((2 * k, p), BF16), vmem((k, t), F32),
            vmem((3, rows, b), F32), vmem((3, n, shard, b), F32), vmem((3, m, shard, b), F32),
            vmem((3, rows, b), F32), vmem((2, n, k, b), F32), vmem((2, m, k, b), F32),
            vmem((3, k, b), F32), vmem((3, 4, k, b), F32),
            sem((a,)), sem((a,)), sem((a,)),
            sem((3, n)), sem((3, n)), sem((3, m)), sem((3, m)), sem((3, n)), sem((3, n)),
            sem((2, n)), sem((2, n)), sem((2, m)), sem((2, m)), sem((3, 4)), sem((3, 4)),
        ],
        compiler_params=pltpu.CompilerParams(
            collective_id=0, has_side_effects=True, vmem_limit_bytes=60 * 1024 * 1024
        ),
        name="power_steps",
    )(snapshots, land_sea, penalty, initial_basis)


def solution(mesh):
    in_specs = (P(None, "lat", "lon"), P("lat", "lon"), P("lat", "lon"), P(None, "lat", "lon"))
    out_specs = (P(None, "lat", "lon"), P())
    return jax.shard_map(local, mesh=mesh, in_specs=in_specs, out_specs=out_specs, check_vma=False)
```

```python
import functools

import jax
import jax.numpy as jnp
from jax import lax
from jax.experimental import pallas as pl
from jax.experimental.pallas import tpu as pltpu
from jax.sharding import PartitionSpec as P

STEPS = 2
MESH = pl.DeviceIdType.MESH
F32 = jnp.float32
BF16 = jnp.bfloat16
NT = (((1,), (1,)), ((), ()))
NN = (((1,), (0,)), ((), ()))


def dot_low(a, b, dims):
    return lax.dot_general(a, b, dims, preferred_element_type=F32)


def dot_full(a, b, dims):
    return lax.dot_general(
        a, b, dims, precision=lax.Precision.HIGHEST, preferred_element_type=F32
    )


def split(x):
    high = x.astype(BF16)
    return high, (x - high.astype(F32)).astype(BF16)


def split3(x):
    high = x.astype(BF16)
    rest = x - high.astype(F32)
    mid = rest.astype(BF16)
    return jnp.concatenate([high, mid, (rest - mid.astype(F32)).astype(BF16)], axis=0)


def fold_rows(x, k):
    return x[:k] + (x[k:2 * k] + x[2 * k:])


def products(left, right):
    k = left.shape[0] // 3
    x = fold_rows(dot_low(left, right, NT), k)
    return x[:, :k] + (x[:, k:2 * k] + x[:, 2 * k:])


def factor_parts(inverse):
    k = inverse.shape[0]
    parts = split3(inverse)
    return jnp.concatenate([parts, parts, parts], axis=1)


def times(parts, right):
    return fold_rows(dot_low(parts, right, NN), parts.shape[0] // 3)


def inverse_factor(gram):
    k = gram.shape[0]
    panel = 4
    rows = lax.broadcasted_iota(jnp.int32, (k, k), 0)
    cols = lax.broadcasted_iota(jnp.int32, (k, k), 1)
    eye = jnp.where(rows == cols, 1.0, 0.0).astype(F32)
    work = jnp.concatenate([gram, eye], axis=1)
    count = k // 8
    shape = (8, 2 * k)
    blocks = [work[8 * i:8 * i + 8] for i in range(count)]
    sub = lax.broadcasted_iota(jnp.int32, shape, 0)
    pivots = [jnp.zeros(shape, F32) for _ in range(count)]
    for j in range(0, k, panel):
        own, at = j // 8, j % 8
        row = [jnp.broadcast_to(blocks[own][at + a:at + a + 1, :], shape) for a in range(panel)]
        column = [
            [jnp.broadcast_to(blocks[i][:, j + a:j + a + 1], shape) for i in range(own, count)]
            for a in range(panel)
        ]
        corner = {
            (b, a): jnp.broadcast_to(column[a][0][at + b:at + b + 1, :], shape)
            for a in range(panel) for b in range(a, panel)
        }
        scaled = []
        for a in range(panel):
            pivot = corner[a, a]
            pivots[own] = jnp.where(sub == at + a, pivot, pivots[own])
            inverse = 1.0 / pivot
            scaled.append(row[a] * inverse)
            factor = {b: corner[b, a] * inverse for b in range(a + 1, panel)}
            for b in range(a + 1, panel):
                for c in range(b, panel):
                    corner[c, b] = corner[c, b] - factor[b] * corner[c, a]
            for b in range(a + 1, panel):
                row[b] = row[b] - factor[b] * row[a]
                column[b] = [y - factor[b] * x for x, y in zip(column[a], column[b])]
        for i in range(own, count):
            change = column[0][i - own] * scaled[0]
            for a in range(1, panel):
                change = change + column[a][i - own] * scaled[a]
            value = blocks[i] - change
            if i == own:
                value = jnp.where(sub >= at + panel, value, blocks[i])
                for a in range(panel):
                    value = jnp.where(sub == at + a, row[a], value)
            blocks[i] = value
    done = [blocks[i] * (1.0 / jnp.sqrt(pivots[i])) for i in range(count)]
    return jnp.concatenate(done, axis=0)[:, k:]


def kernel(
    n, m, points, s_hbm, land_ref, pen_ref, v_hbm, out_hbm, ray_ref,
    s_full, s_high, s_mid, field0, field1, field2, lap_ref, out_buf, v_split, acc,
    cbuf, rs, zr, fin, gl, gz, edge, halo,
    s_sem, v_sem, o_sem, rs_s, rs_r, z_s, z_r, ag_s, ag_r, gl_s, gl_r, gz_s, gz_r, h_s, h_r,
):
    lat = lax.axis_index("lat")
    lon = lax.axis_index("lon")
    t_count, a_count, b_count = s_hbm.shape
    k = v_hbm.shape[0]
    fields = (field0, field1, field2)
    shard = cbuf.shape[1] // n
    inverse_points = 1.0 / points
    pending = []

    def part(a):
        return pl.ds(a * b_count, b_count)

    loads = []
    for a in range(a_count):
        loads.append(pltpu.make_async_copy(v_hbm.at[:, a, :], out_buf.at[:, part(a)], v_sem.at[a]))
    for a in range(a_count):
        loads.append(pltpu.make_async_copy(s_hbm.at[:, a, :], s_full.at[:, part(a)], s_sem.at[a]))
    for copy in loads:
        copy.start()

    barrier = pltpu.get_barrier_semaphore()
    for d in range(1, n):
        pl.semaphore_signal(
            barrier, inc=1, device_id=(lax.rem(lat + d, n), lon), device_id_type=MESH
        )
    for e in range(1, m):
        pl.semaphore_signal(
            barrier, inc=1, device_id=(lat, lax.rem(lon + e, m)), device_id_type=MESH
        )
    pl.semaphore_wait(barrier, n + m - 2)

    def send(src, dst, s_s, s_r, where):
        copy = pltpu.make_async_remote_copy(
            src_ref=src, dst_ref=dst, send_sem=s_s, recv_sem=s_r,
            device_id=where, device_id_type=MESH,
        )
        copy.start()
        pending.append(copy)
        return copy

    def to_lat(d):
        return (lax.rem(lat + d, n), lon)

    def to_lon(e):
        return (lat, lax.rem(lon + e, m))

    lane = lax.broadcasted_iota(jnp.int32, (k, b_count), 1)

    def mask_row(a):
        return land_ref[a:a + 1, :].astype(F32)

    def start_halo(r):
        x = fields[r]
        packed = jnp.zeros((k, b_count), F32)
        for a in range(a_count):
            block = x[:, a * b_count:(a + 1) * b_count]
            low = block if a == 0 else pltpu.roll(block, a, axis=1)
            high = pltpu.roll(block, a_count + a + 1, axis=1)
            packed = jnp.where(lane == a, low, packed)
            packed = jnp.where(lane == a_count + a, high, packed)
        edge[r] = packed
        return [
            send(x.at[:, part(a_count - 1)], halo.at[r, 0], h_s.at[r, 0], h_r.at[r, 0], to_lat(1)),
            send(x.at[:, part(0)], halo.at[r, 1], h_s.at[r, 1], h_r.at[r, 1], to_lat(n - 1)),
            send(edge.at[r], halo.at[r, 2], h_s.at[r, 2], h_r.at[r, 2], to_lon(1)),
            send(edge.at[r], halo.at[r, 3], h_s.at[r, 3], h_r.at[r, 3], to_lon(m - 1)),
        ]

    def laplacian(r, copies):
        for copy in copies:
            copy.wait_recv()
        x = fields[r]
        above = jnp.where(lat > 0, halo[r, 0], 0.0)
        below = jnp.where(lat < n - 1, halo[r, 1], 0.0)
        west = jnp.where(lon > 0, halo[r, 2], 0.0)
        east = jnp.where(lon < m - 1, halo[r, 3], 0.0)
        for a in range(a_count):
            block = x[:, a * b_count:(a + 1) * b_count]
            up = above if a == 0 else x[:, (a - 1) * b_count:a * b_count]
            down = below if a == a_count - 1 else x[:, (a + 1) * b_count:(a + 2) * b_count]
            left = jnp.where(
                lane == 0, pltpu.roll(west, b_count - a_count - a, axis=1),
                pltpu.roll(block, 1, axis=1),
            )
            right = jnp.where(
                lane == b_count - 1, pltpu.roll(east, b_count - 1 - a, axis=1),
                pltpu.roll(block, b_count - 1, axis=1),
            )
            total = (down + up + right + left) - 4.0 * block
            lap_ref[:, a * b_count:(a + 1) * b_count] = total * pen_ref[a:a + 1, :]

    def store_field(r, a, value):
        x = value * mask_row(a)
        at = slice(a * b_count, (a + 1) * b_count)
        fields[r][:, at] = x
        v_split[:, at] = split3(x)

    def store_coeffs(r, block, value):
        for w in range(value.shape[1] // b_count):
            row = (block * (value.shape[1] // b_count) + w) * k
            cbuf[r, row:row + k, :] = value[:, w * b_count:(w + 1) * b_count]

    def start_scatter(r):
        copies = []
        for d in range(1, n):
            there = lax.rem(lat + d, n)
            rows = pl.ds(pl.multiple_of(there * shard, shard), shard)
            copies.append(
                send(cbuf.at[r, rows], rs.at[r, d], rs_s.at[r, d], rs_r.at[r, d], to_lat(d))
            )
        return copies

    def own_rows():
        return pl.ds(pl.multiple_of(lat * shard, shard), shard)

    def finish_scatter(r, copies):
        total = cbuf[r, own_rows(), :]
        for d, copy in enumerate(copies):
            copy.wait_recv()
            total = total + rs[r, d + 1]
        zr[r, lon] = total
        return [
            send(zr.at[r, lon], zr.at[r, lon], z_s.at[r, e], z_r.at[r, e], to_lon(e))
            for e in range(1, m)
        ]

    def start_gather(r, copies):
        for copy in copies:
            copy.wait_recv()
        total = zr[r, 0]
        for e in range(1, m):
            total = total + zr[r, e]
        fin[r, own_rows(), :] = total
        return [
            send(fin.at[r, own_rows()], fin.at[r, own_rows()], ag_s.at[r, d], ag_r.at[r, d], to_lat(d))
            for d in range(1, n)
        ]

    def finish_gather(r, copies):
        for copy in copies:
            copy.wait_recv()
        return jnp.concatenate(
            [fin[r, i * k:(i + 1) * k, :] for i in range(t_count // b_count)], axis=1
        )

    def start_gram(r, value):
        gl[r, lat] = value
        return [
            send(gl.at[r, lat], gl.at[r, lat], gl_s.at[r, d], gl_r.at[r, d], to_lat(d))
            for d in range(1, n)
        ]

    def middle_gram(r, copies):
        for copy in copies:
            copy.wait_recv()
        total = gl[r, 0]
        for d in range(1, n):
            total = total + gl[r, d]
        gz[r, lon] = total
        return [
            send(gz.at[r, lon], gz.at[r, lon], gz_s.at[r, e], gz_r.at[r, e], to_lon(e))
            for e in range(1, m)
        ]

    def finish_gram(r, copies):
        for copy in copies:
            copy.wait_recv()
        total = gz[r, 0]
        for e in range(1, m):
            total = total + gz[r, e]
        return total

    def project(r):
        width = 2 * b_count
        for block in range(t_count // width):
            rows = slice(block * width, (block + 1) * width)
            both = dot_low(v_split[:2 * k, :], s_high[rows, :], NT)
            rest = dot_low(v_split[:k, :], s_mid[rows, :], NT)
            store_coeffs(r, block, both[:k] + (both[k:] + rest))

    def expand(r, coeffs):
        high, mid = split(coeffs)
        stacked = jnp.concatenate([high, mid], axis=0)
        width = 2 * b_count
        for block in range(a_count // 2):
            at = slice(block * width, (block + 1) * width)
            both = dot_low(stacked, s_high[:, at], NN)
            rest = dot_low(high, s_mid[:, at], NN)
            value = (both[:k] + (both[k:] + rest)) * inverse_points + lap_ref[:, at]
            store_field(r, 2 * block, value[:, :b_count])
            store_field(r, 2 * block + 1, value[:, b_count:])

    for a in range(a_count):
        loads[a].wait()
        store_field(0, a, out_buf[:, a * b_count:(a + 1) * b_count])
    halo_copies = start_halo(0)
    width = 2 * b_count
    for block in range(a_count // 2):
        at = slice(block * width, (block + 1) * width)
        loads[a_count + 2 * block].wait()
        loads[a_count + 2 * block + 1].wait()
        high, mid = split(s_full[:, at])
        s_high[:, at] = high
        s_mid[:, at] = mid
        both = dot_low(v_split[:2 * k, at], high, NT)
        rest = dot_low(v_split[:k, at], mid, NT)
        value = both[:k] + (both[k:] + rest)
        if block == 0:
            acc[...] = value
        else:
            acc[...] += value
    store_coeffs(0, 0, acc[...])
    copies = start_scatter(0)
    laplacian(0, halo_copies)
    copies = finish_scatter(0, copies)
    copies = start_gather(0, copies)
    expand(1, finish_gather(0, copies))

    halo_copies = start_halo(1)
    gram = products(v_split[...], v_split[...]) * inverse_points
    gram_copies = start_gram(0, jnp.concatenate([gram, gram], axis=1))
    project(1)
    copies = start_scatter(1)
    gram_copies = middle_gram(0, gram_copies)
    laplacian(1, halo_copies)
    copies = finish_scatter(1, copies)
    parts = factor_parts(inverse_factor(finish_gram(0, gram_copies)[:, :k]))
    copies = start_gather(1, copies)
    lap_ref[...] = times(parts, split3(lap_ref[...]))
    expand(2, times(parts, split3(finish_gather(1, copies))))

    halo_copies = start_halo(2)
    project(2)
    copies = start_scatter(2)
    laplacian(2, halo_copies)
    gram = products(v_split[...], v_split[...]) * inverse_points
    rough = products(v_split[...], split3(lap_ref[...]))
    gram_copies = start_gram(1, jnp.concatenate([gram, rough], axis=1))
    copies = finish_scatter(2, copies)
    gram_copies = middle_gram(1, gram_copies)
    copies = start_gather(2, copies)
    both = finish_gram(1, gram_copies)
    inverse = inverse_factor(both[:, :k])
    parts = factor_parts(inverse)
    stores = []
    for a in range(a_count):
        at = slice(a * b_count, (a + 1) * b_count)
        out_buf[:, at] = times(parts, v_split[:, at])
        copy = pltpu.make_async_copy(out_buf.at[:, part(a)], out_hbm.at[:, a, :], o_sem.at[a])
        copy.start()
        stores.append(copy)
    coeffs = finish_gather(2, copies)
    coeffs = split3(coeffs)
    middle = products(coeffs, coeffs) * inverse_points + both[:, k:]
    ray_ref[...] = dot_full(dot_full(inverse, middle, NN), inverse, NT) * inverse_points
    for copy in stores:
        copy.wait()
    for copy in pending:
        copy.wait_send()


def local(snapshots, land_sea, penalty, initial_basis):
    n, m = lax.axis_size("lat"), lax.axis_size("lon")
    t, a, b = snapshots.shape
    k = initial_basis.shape[0]
    points = float(a * b * n * m)
    p = a * b
    rows = t * k // b
    shard = rows // n
    sem = pltpu.SemaphoreType.DMA
    vmem = pltpu.VMEM
    any_spec = pl.BlockSpec(memory_space=pl.ANY)
    vmem_spec = pl.BlockSpec(memory_space=pltpu.VMEM)
    return pl.pallas_call(
        functools.partial(kernel, n, m, points),
        out_shape=(
            jax.ShapeDtypeStruct((k, a, b), F32),
            jax.ShapeDtypeStruct((k, k), F32),
        ),
        in_specs=[any_spec, vmem_spec, vmem_spec, any_spec],
        out_specs=(any_spec, vmem_spec),
        scratch_shapes=[
            vmem((t, p), F32), vmem((t, p), BF16), vmem((t, p), BF16),
            vmem((k, p), F32), vmem((k, p), F32), vmem((k, p), F32),
            vmem((k, p), F32), vmem((k, p), F32), vmem((3 * k, p), BF16), vmem((k, t), F32),
            vmem((3, rows, b), F32), vmem((3, n, shard, b), F32), vmem((3, m, shard, b), F32),
            vmem((3, rows, b), F32), vmem((2, n, k, b), F32), vmem((2, m, k, b), F32),
            vmem((3, k, b), F32), vmem((3, 4, k, b), F32),
            sem((a,)), sem((a,)), sem((a,)),
            sem((3, n)), sem((3, n)), sem((3, m)), sem((3, m)), sem((3, n)), sem((3, n)),
            sem((2, n)), sem((2, n)), sem((2, m)), sem((2, m)), sem((3, 4)), sem((3, 4)),
        ],
        compiler_params=pltpu.CompilerParams(
            collective_id=0, has_side_effects=True, vmem_limit_bytes=60 * 1024 * 1024
        ),
        name="power_steps",
    )(snapshots, land_sea, penalty, initial_basis)


def solution(mesh):
    in_specs = (P(None, "lat", "lon"), P("lat", "lon"), P("lat", "lon"), P(None, "lat", "lon"))
    out_specs = (P(None, "lat", "lon"), P())
    return jax.shard_map(local, mesh=mesh, in_specs=in_specs, out_specs=out_specs, check_vma=False)
```

```python
import functools

import jax
import jax.numpy as jnp
from jax import lax
from jax.experimental import pallas as pl
from jax.experimental.pallas import tpu as pltpu
from jax.sharding import PartitionSpec as P

STEPS = 2
MESH = pl.DeviceIdType.MESH
F32 = jnp.float32
BF16 = jnp.bfloat16
NT = (((1,), (1,)), ((), ()))
NN = (((1,), (0,)), ((), ()))


def dot_low(a, b, dims):
    return lax.dot_general(a, b, dims, preferred_element_type=F32)


def dot_full(a, b, dims):
    return lax.dot_general(
        a, b, dims, precision=lax.Precision.HIGHEST, preferred_element_type=F32
    )


def split(x):
    high = x.astype(BF16)
    return high, (x - high.astype(F32)).astype(BF16)


def split3(x):
    high = x.astype(BF16)
    rest = x - high.astype(F32)
    mid = rest.astype(BF16)
    return jnp.concatenate([high, mid, (rest - mid.astype(F32)).astype(BF16)], axis=0)


def fold_rows(x, k):
    return x[:k] + (x[k:2 * k] + x[2 * k:])


def products(left, right):
    k = left.shape[0] // 3
    x = fold_rows(dot_low(left, right, NT), k)
    return x[:, :k] + (x[:, k:2 * k] + x[:, 2 * k:])


def factor_parts(inverse):
    k = inverse.shape[0]
    parts = split3(inverse)
    return jnp.concatenate([parts, parts, parts], axis=1)


def times(parts, right):
    return fold_rows(dot_low(parts, right, NN), parts.shape[0] // 3)


def inverse_factor(gram):
    k = gram.shape[0]
    panel = 4
    rows = lax.broadcasted_iota(jnp.int32, (k, k), 0)
    cols = lax.broadcasted_iota(jnp.int32, (k, k), 1)
    eye = jnp.where(rows == cols, 1.0, 0.0).astype(F32)
    work = jnp.concatenate([gram, eye], axis=1)
    count = k // 8
    shape = (8, 2 * k)
    blocks = [work[8 * i:8 * i + 8] for i in range(count)]
    sub = lax.broadcasted_iota(jnp.int32, shape, 0)
    pivots = [jnp.zeros(shape, F32) for _ in range(count)]
    for j in range(0, k, panel):
        own, at = j // 8, j % 8
        row = [jnp.broadcast_to(blocks[own][at + a:at + a + 1, :], shape) for a in range(panel)]
        column = [
            [jnp.broadcast_to(blocks[i][:, j + a:j + a + 1], shape) for i in range(own, count)]
            for a in range(panel)
        ]
        corner = {
            (b, a): jnp.broadcast_to(column[a][0][at + b:at + b + 1, :], shape)
            for a in range(panel) for b in range(a, panel)
        }
        scaled = []
        for a in range(panel):
            pivot = corner[a, a]
            pivots[own] = jnp.where(sub == at + a, pivot, pivots[own])
            inverse = 1.0 / pivot
            scaled.append(row[a] * inverse)
            factor = {b: corner[b, a] * inverse for b in range(a + 1, panel)}
            for b in range(a + 1, panel):
                for c in range(b, panel):
                    corner[c, b] = corner[c, b] - factor[b] * corner[c, a]
            for b in range(a + 1, panel):
                row[b] = row[b] - factor[b] * row[a]
                column[b] = [y - factor[b] * x for x, y in zip(column[a], column[b])]
        for i in range(own, count):
            change = column[0][i - own] * scaled[0]
            for a in range(1, panel):
                change = change + column[a][i - own] * scaled[a]
            value = blocks[i] - change
            if i == own:
                value = jnp.where(sub >= at + panel, value, blocks[i])
                for a in range(panel):
                    value = jnp.where(sub == at + a, row[a], value)
            blocks[i] = value
    done = [blocks[i] * (1.0 / jnp.sqrt(pivots[i])) for i in range(count)]
    return jnp.concatenate(done, axis=0)[:, k:]


def kernel(
    n, m, points, s_hbm, land_ref, pen_ref, v_hbm, out_hbm, ray_ref,
    s_full, s_high, s_mid, field0, field1, field2, lap_ref, out_buf, v_split, acc,
    cbuf, rs, zr, fin, gl, gz, edge, halo,
    s_sem, v_sem, o_sem, rs_s, rs_r, z_s, z_r, ag_s, ag_r, gl_s, gl_r, gz_s, gz_r, h_s, h_r,
):
    lat = lax.axis_index("lat")
    lon = lax.axis_index("lon")
    t_count, a_count, b_count = s_hbm.shape
    k = v_hbm.shape[0]
    fields = (field0, field1, field2)
    shard = cbuf.shape[1] // n
    half = shard // 2
    inverse_points = 1.0 / points
    pending = []

    def part(a):
        return pl.ds(a * b_count, b_count)

    loads = []
    for a in range(a_count):
        loads.append(pltpu.make_async_copy(v_hbm.at[:, a, :], out_buf.at[:, part(a)], v_sem.at[a]))
    for a in range(a_count):
        loads.append(pltpu.make_async_copy(s_hbm.at[:, a, :], s_full.at[:, part(a)], s_sem.at[a]))
    for copy in loads:
        copy.start()

    barrier = pltpu.get_barrier_semaphore()
    for d in range(1, n):
        pl.semaphore_signal(
            barrier, inc=1, device_id=(lax.rem(lat + d, n), lon), device_id_type=MESH
        )
    for e in range(1, m):
        pl.semaphore_signal(
            barrier, inc=1, device_id=(lat, lax.rem(lon + e, m)), device_id_type=MESH
        )
    pl.semaphore_wait(barrier, n + m - 2)

    def send(src, dst, s_s, s_r, where):
        copy = pltpu.make_async_remote_copy(
            src_ref=src, dst_ref=dst, send_sem=s_s, recv_sem=s_r,
            device_id=where, device_id_type=MESH,
        )
        copy.start()
        pending.append(copy)
        return copy

    def to_lat(d):
        return (lax.rem(lat + d, n), lon)

    def to_lon(e):
        return (lat, lax.rem(lon + e, m))

    lane = lax.broadcasted_iota(jnp.int32, (k, b_count), 1)

    def mask_row(a):
        return land_ref[a:a + 1, :].astype(F32)

    def start_halo(r):
        x = fields[r]
        packed = jnp.zeros((k, b_count), F32)
        for a in range(a_count):
            block = x[:, a * b_count:(a + 1) * b_count]
            low = block if a == 0 else pltpu.roll(block, a, axis=1)
            high = pltpu.roll(block, a_count + a + 1, axis=1)
            packed = jnp.where(lane == a, low, packed)
            packed = jnp.where(lane == a_count + a, high, packed)
        edge[r] = packed
        return [
            send(x.at[:, part(a_count - 1)], halo.at[r, 0], h_s.at[r, 0], h_r.at[r, 0], to_lat(1)),
            send(x.at[:, part(0)], halo.at[r, 1], h_s.at[r, 1], h_r.at[r, 1], to_lat(n - 1)),
            send(edge.at[r], halo.at[r, 2], h_s.at[r, 2], h_r.at[r, 2], to_lon(1)),
            send(edge.at[r], halo.at[r, 3], h_s.at[r, 3], h_r.at[r, 3], to_lon(m - 1)),
        ]

    def laplacian(r, copies):
        for copy in copies:
            copy.wait_recv()
        x = fields[r]
        above = jnp.where(lat > 0, halo[r, 0], 0.0)
        below = jnp.where(lat < n - 1, halo[r, 1], 0.0)
        west = jnp.where(lon > 0, halo[r, 2], 0.0)
        east = jnp.where(lon < m - 1, halo[r, 3], 0.0)
        for a in range(a_count):
            block = x[:, a * b_count:(a + 1) * b_count]
            up = above if a == 0 else x[:, (a - 1) * b_count:a * b_count]
            down = below if a == a_count - 1 else x[:, (a + 1) * b_count:(a + 2) * b_count]
            left = jnp.where(
                lane == 0, pltpu.roll(west, b_count - a_count - a, axis=1),
                pltpu.roll(block, 1, axis=1),
            )
            right = jnp.where(
                lane == b_count - 1, pltpu.roll(east, b_count - 1 - a, axis=1),
                pltpu.roll(block, b_count - 1, axis=1),
            )
            total = (down + up + right + left) - 4.0 * block
            lap_ref[:, a * b_count:(a + 1) * b_count] = total * pen_ref[a:a + 1, :]

    def store_field(r, a, value):
        x = value * mask_row(a)
        at = slice(a * b_count, (a + 1) * b_count)
        fields[r][:, at] = x
        v_split[:, at] = split3(x)

    def store_coeffs(r, block, value):
        for w in range(value.shape[1] // b_count):
            row = (block * (value.shape[1] // b_count) + w) * k
            cbuf[r, row:row + k, :] = value[:, w * b_count:(w + 1) * b_count]

    def band_rows(owner, h):
        return pl.ds(pl.multiple_of(owner * shard + h * half, half), half)

    def start_scatter(r):
        copies = []
        for h in range(2):
            into = pl.ds(h * half, half)
            copies.append([
                send(
                    cbuf.at[r, band_rows(lax.rem(lat + d, n), h)], rs.at[r, d, into],
                    rs_s.at[r, h, d], rs_r.at[r, h, d], to_lat(d),
                )
                for d in range(1, n)
            ])
        return copies

    def finish_scatter(r, copies):
        sends = []
        for h in range(2):
            into = pl.ds(h * half, half)
            total = cbuf[r, band_rows(lat, h), :]
            for d, copy in enumerate(copies[h]):
                copy.wait_recv()
                total = total + rs[r, d + 1, h * half:(h + 1) * half, :]
            zr[r, lon, h * half:(h + 1) * half, :] = total
            sends.append([
                send(
                    zr.at[r, lon, into], zr.at[r, lon, into],
                    z_s.at[r, h, e], z_r.at[r, h, e], to_lon(e),
                )
                for e in range(1, m)
            ])
        return sends

    def start_gather(r, copies):
        sends = []
        for h in range(2):
            for copy in copies[h]:
                copy.wait_recv()
            total = zr[r, 0, h * half:(h + 1) * half, :]
            for e in range(1, m):
                total = total + zr[r, e, h * half:(h + 1) * half, :]
            fin[r, band_rows(lat, h), :] = total
            sends.extend(
                send(
                    fin.at[r, band_rows(lat, h)], fin.at[r, band_rows(lat, h)],
                    ag_s.at[r, h, d], ag_r.at[r, h, d], to_lat(d),
                )
                for d in range(1, n)
            )
        return sends

    def finish_gather(r, copies):
        for copy in copies:
            copy.wait_recv()
        return jnp.concatenate(
            [fin[r, i * k:(i + 1) * k, :] for i in range(t_count // b_count)], axis=1
        )

    def start_gram(r, value):
        gl[r, lat] = value
        return [
            send(gl.at[r, lat], gl.at[r, lat], gl_s.at[r, d], gl_r.at[r, d], to_lat(d))
            for d in range(1, n)
        ]

    def middle_gram(r, copies):
        for copy in copies:
            copy.wait_recv()
        total = gl[r, 0]
        for d in range(1, n):
            total = total + gl[r, d]
        gz[r, lon] = total
        return [
            send(gz.at[r, lon], gz.at[r, lon], gz_s.at[r, e], gz_r.at[r, e], to_lon(e))
            for e in range(1, m)
        ]

    def finish_gram(r, copies):
        for copy in copies:
            copy.wait_recv()
        total = gz[r, 0]
        for e in range(1, m):
            total = total + gz[r, e]
        return total

    def project(r):
        width = 2 * b_count
        for block in range(t_count // width):
            rows = slice(block * width, (block + 1) * width)
            both = dot_low(v_split[:2 * k, :], s_high[rows, :], NT)
            rest = dot_low(v_split[:k, :], s_mid[rows, :], NT)
            store_coeffs(r, block, both[:k] + (both[k:] + rest))

    def expand(r, coeffs):
        high, mid = split(coeffs)
        stacked = jnp.concatenate([high, mid], axis=0)
        width = 2 * b_count
        for block in range(a_count // 2):
            at = slice(block * width, (block + 1) * width)
            both = dot_low(stacked, s_high[:, at], NN)
            rest = dot_low(high, s_mid[:, at], NN)
            value = (both[:k] + (both[k:] + rest)) * inverse_points + lap_ref[:, at]
            store_field(r, 2 * block, value[:, :b_count])
            store_field(r, 2 * block + 1, value[:, b_count:])

    for a in range(a_count):
        loads[a].wait()
        store_field(0, a, out_buf[:, a * b_count:(a + 1) * b_count])
    halo_copies = start_halo(0)
    width = 2 * b_count
    for block in range(a_count // 2):
        at = slice(block * width, (block + 1) * width)
        loads[a_count + 2 * block].wait()
        loads[a_count + 2 * block + 1].wait()
        high, mid = split(s_full[:, at])
        s_high[:, at] = high
        s_mid[:, at] = mid
        both = dot_low(v_split[:2 * k, at], high, NT)
        rest = dot_low(v_split[:k, at], mid, NT)
        value = both[:k] + (both[k:] + rest)
        if block == 0:
            acc[...] = value
        else:
            acc[...] += value
    store_coeffs(0, 0, acc[...])
    copies = start_scatter(0)
    laplacian(0, halo_copies)
    copies = finish_scatter(0, copies)
    copies = start_gather(0, copies)
    expand(1, finish_gather(0, copies))

    halo_copies = start_halo(1)
    gram = products(v_split[...], v_split[...]) * inverse_points
    gram_copies = start_gram(0, jnp.concatenate([gram, gram], axis=1))
    project(1)
    copies = start_scatter(1)
    gram_copies = middle_gram(0, gram_copies)
    laplacian(1, halo_copies)
    copies = finish_scatter(1, copies)
    parts = factor_parts(inverse_factor(finish_gram(0, gram_copies)[:, :k]))
    copies = start_gather(1, copies)
    lap_ref[...] = times(parts, split3(lap_ref[...]))
    expand(2, times(parts, split3(finish_gather(1, copies))))

    halo_copies = start_halo(2)
    project(2)
    copies = start_scatter(2)
    laplacian(2, halo_copies)
    gram = products(v_split[...], v_split[...]) * inverse_points
    rough = products(v_split[...], split3(lap_ref[...]))
    gram_copies = start_gram(1, jnp.concatenate([gram, rough], axis=1))
    copies = finish_scatter(2, copies)
    gram_copies = middle_gram(1, gram_copies)
    copies = start_gather(2, copies)
    both = finish_gram(1, gram_copies)
    inverse = inverse_factor(both[:, :k])
    parts = factor_parts(inverse)
    stores = []
    for a in range(a_count):
        at = slice(a * b_count, (a + 1) * b_count)
        out_buf[:, at] = times(parts, v_split[:, at])
        copy = pltpu.make_async_copy(out_buf.at[:, part(a)], out_hbm.at[:, a, :], o_sem.at[a])
        copy.start()
        stores.append(copy)
    coeffs = finish_gather(2, copies)
    coeffs = split3(coeffs)
    middle = products(coeffs, coeffs) * inverse_points + both[:, k:]
    ray_ref[...] = dot_full(dot_full(inverse, middle, NN), inverse, NT) * inverse_points
    for copy in stores:
        copy.wait()
    for copy in pending:
        copy.wait_send()


def local(snapshots, land_sea, penalty, initial_basis):
    n, m = lax.axis_size("lat"), lax.axis_size("lon")
    t, a, b = snapshots.shape
    k = initial_basis.shape[0]
    points = float(a * b * n * m)
    p = a * b
    rows = t * k // b
    shard = rows // n
    sem = pltpu.SemaphoreType.DMA
    vmem = pltpu.VMEM
    any_spec = pl.BlockSpec(memory_space=pl.ANY)
    vmem_spec = pl.BlockSpec(memory_space=pltpu.VMEM)
    return pl.pallas_call(
        functools.partial(kernel, n, m, points),
        out_shape=(
            jax.ShapeDtypeStruct((k, a, b), F32),
            jax.ShapeDtypeStruct((k, k), F32),
        ),
        in_specs=[any_spec, vmem_spec, vmem_spec, any_spec],
        out_specs=(any_spec, vmem_spec),
        scratch_shapes=[
            vmem((t, p), F32), vmem((t, p), BF16), vmem((t, p), BF16),
            vmem((k, p), F32), vmem((k, p), F32), vmem((k, p), F32),
            vmem((k, p), F32), vmem((k, p), F32), vmem((3 * k, p), BF16), vmem((k, t), F32),
            vmem((3, rows, b), F32), vmem((3, n, shard, b), F32), vmem((3, m, shard, b), F32),
            vmem((3, rows, b), F32), vmem((2, n, k, b), F32), vmem((2, m, k, b), F32),
            vmem((3, k, b), F32), vmem((3, 4, k, b), F32),
            sem((a,)), sem((a,)), sem((a,)),
            sem((3, 2, n)), sem((3, 2, n)), sem((3, 2, m)), sem((3, 2, m)), sem((3, 2, n)), sem((3, 2, n)),
            sem((2, n)), sem((2, n)), sem((2, m)), sem((2, m)), sem((3, 4)), sem((3, 4)),
        ],
        compiler_params=pltpu.CompilerParams(
            collective_id=0, has_side_effects=True, vmem_limit_bytes=60 * 1024 * 1024
        ),
        name="power_steps",
    )(snapshots, land_sea, penalty, initial_basis)


def solution(mesh):
    in_specs = (P(None, "lat", "lon"), P("lat", "lon"), P("lat", "lon"), P(None, "lat", "lon"))
    out_specs = (P(None, "lat", "lon"), P())
    return jax.shard_map(local, mesh=mesh, in_specs=in_specs, out_specs=out_specs, check_vma=False)
```
